512 devices in a mesh: seq: 32 (over y, x), doc: 16 (over z, core).
Axes of the slice: x: 4, y: 8, z: 8, core: 2. Of those that a mesh axis runs over, the one named last changes fastest.
Arguments:
- teacher: bfloat16 [16, 4096, 4096], P('doc', 'seq'), may hold values from -24 to 24
- student: bfloat16 [16, 4096, 3072], P('doc', 'seq'), may hold values from -6 to 6
- adapter: bfloat16 [4096, 128], P(('seq', 'doc')), may hold values from -0.09375 to 0.09375
- up_weight: bfloat16 [128, 3072], replicated, may hold values from -0.53033009 to 0.53033009
- band_start: int32 [16, 4096], P('doc', 'seq'), may hold values from 0 to 4095, as said below
- band_len: int32 [16, 4096], P('doc', 'seq'), may hold values from 1 to 64, as said below
Outputs:
- student_grad: bfloat16 [16, 4096, 3072], P('doc', 'seq')
- adapter_grad: float32 [4096, 128], P(('seq', 'doc'))
- up_grad: float32 [128, 3072], P(None, 'doc')
- loss: float32 [], replicated
The draws below stay inside these ranges and needn't reach their ends.
Inputs may be any that keep to these rules, and one draw needn't show every extreme that they name: For student token i the band lies inside the document and inside teacher rows 128 * (i // 128) - 64 to 128 * (i // 128 + 1) + 128 // 2 - 1; band_start + band_len <= 4096; the last student token of every document has the single band row 4095. `band_len`: some token of every document has a band of exactly 64 rows.
All inputs are finite; a program needn't handle non-finite values.
Results may differ from the reference program's by a relative error of at most 0.0083.
The reference program's roundings to bfloat16 on the way count: a program that leaves them out, or rounds other values in their place, can miss the bound.
Values may be sent and summed in bfloat16 or wider, within the bound.
A program may use at most 64 MiB of HBM per device.

```python
import jax
import jax.numpy as jnp
from jax import lax

TD = 4096
SD = 3072
RANK = 128
BAND = 64
TOK_DEV = 128
TOKENS = 4096
DOCS = 16
N_SEQ = 32


spike_factor = 4.0


def band_pair(key):
    first_key, second_key = jax.random.split(jax.random.fold_in(key, 11))
    lengths = jax.random.randint(first_key, (DOCS, TOKENS), 1, BAND + 1, dtype=jnp.int32)
    lengths = lengths.at[:, 0].set(BAND)
    lengths = lengths.at[:, TOKENS - 1].set(1)
    reach = TOK_DEV // 2 - BAND // 2 - 1
    wander = jax.random.randint(second_key, (DOCS, TOKENS), -reach, reach + 1, dtype=jnp.int32)
    centre = jnp.arange(TOKENS, dtype=jnp.int32)[None, :] + wander
    firsts = jnp.clip(centre - lengths // 2, 0, TOKENS - lengths)
    firsts = firsts.at[:, TOKENS - 1].set(TOKENS - 1)
    return (firsts.astype(jnp.int32), lengths.astype(jnp.int32))


def draw_band_start(key, part):
    return band_pair(key)[0]


def draw_band_len(key, part):
    return band_pair(key)[1]


def draw_student(key, part):
    noise_key = jax.random.fold_in(jax.random.fold_in(key, 31), 0)
    values = jnp.clip(jax.random.normal(noise_key, (DOCS, TOKENS, SD), jnp.float32), -6.0, 6.0)
    return values.astype(jnp.bfloat16)


def draw_up_weight(key, part):
    rest_key = jax.random.fold_in(jax.random.fold_in(key, 37), 0)
    sigma = RANK ** (-0.5)
    values = sigma * jnp.clip(jax.random.normal(rest_key, (RANK, SD), jnp.float32), -6.0, 6.0)
    return values.astype(jnp.bfloat16)


def draw_adapter(key, part):
    rest_key = jax.random.fold_in(jax.random.fold_in(key, 41), 0)
    sigma = TD ** (-0.5)
    values = sigma * jnp.clip(jax.random.normal(rest_key, (TD, RANK), jnp.float32), -6.0, 6.0)
    return values.astype(jnp.bfloat16)


def draw_teacher(key, part):
    noise_key, pair_key = jax.random.split(jax.random.fold_in(key, 47))
    shard_count = TOKENS // TOK_DEV
    owners = DOCS * shard_count
    block_width = TD // owners
    order = jax.random.permutation(pair_key, owners).astype(jnp.int32)
    row_owner = jnp.repeat(order.reshape(DOCS, shard_count), TOK_DEV, axis=1)
    column_block = jnp.arange(TD, dtype=jnp.int32) // block_width
    paired = row_owner[:, :, None] == column_block[None, None, :]
    factor = jnp.where(paired, spike_factor, 1.0)
    values = jnp.clip(jax.random.normal(noise_key, (DOCS, TOKENS, TD), jnp.float32), -6.0, 6.0) * factor
    return values.astype(jnp.bfloat16)


def setup_inputs(seed: int = 0) -> dict:
    keys = jax.random.split(jax.random.key(seed), 7)
    teacher = draw_teacher(jax.random.fold_in(keys[6], 71), 0)
    student = draw_student(jax.random.fold_in(keys[6], 71), 0)
    adapter = draw_adapter(jax.random.fold_in(keys[6], 71), 0)
    up_weight = draw_up_weight(jax.random.fold_in(keys[6], 71), 0)
    band_start = draw_band_start(jax.random.fold_in(keys[6], 71), 0)
    band_len = draw_band_len(jax.random.fold_in(keys[6], 71), 0)
    return {"teacher": teacher, "student": student, "adapter": adapter, "up_weight": up_weight, "band_start": band_start, "band_len": band_len}


def contract_rows(left, right):
    return lax.dot_general(left, right, (((0,), (0,)), ((), ())), preferred_element_type=jnp.float32)


def contract_cols(left, right):
    return lax.dot_general(left, right, (((1,), (1,)), ((), ())), preferred_element_type=jnp.float32)


def band_pass(student_rows, key_rows, firsts, lengths, up_weight, row_first):
    scale = student_rows.shape[1] ** -0.5
    query = contract_cols(student_rows, up_weight).astype(jnp.bfloat16)
    scores = contract_cols(query, key_rows) * scale
    position = row_first + jnp.arange(key_rows.shape[0], dtype=jnp.int32)
    inside = (position[None, :] >= firsts[:, None]) & (position[None, :] < (firsts + lengths)[:, None])
    scores = jnp.where(inside, scores, -1e30)
    row_max = jnp.max(scores, axis=1, keepdims=True)
    weights = jnp.where(inside, jnp.exp(scores - row_max), 0.0)
    prob = weights / jnp.sum(weights, axis=1, keepdims=True)
    prob_b = prob.astype(jnp.bfloat16)
    context = jnp.dot(prob_b, key_rows, preferred_element_type=jnp.float32).astype(jnp.bfloat16)
    output = jnp.dot(context, up_weight, preferred_element_type=jnp.float32)
    residual = student_rows.astype(jnp.float32) - output
    loss_part = 0.5 * jnp.sum(residual * residual)
    out_grad = (-residual).astype(jnp.bfloat16)
    ctx_grad = contract_cols(out_grad, up_weight).astype(jnp.bfloat16)
    prob_grad = contract_cols(ctx_grad, key_rows)
    centred = prob_grad - jnp.sum(prob * prob_grad, axis=1, keepdims=True)
    score_grad = (prob * centred * scale).astype(jnp.bfloat16)
    key_grad = (contract_rows(prob_b, ctx_grad) + contract_rows(score_grad, query)).astype(jnp.bfloat16)
    query_grad = jnp.dot(score_grad, key_rows, preferred_element_type=jnp.float32).astype(jnp.bfloat16)
    up_part = contract_rows(context, out_grad) + contract_rows(query_grad, student_rows)
    student_grad = (residual + jnp.dot(query_grad, up_weight, preferred_element_type=jnp.float32)).astype(jnp.bfloat16)
    return student_grad, key_grad, up_part, loss_part


def reference(teacher, student, adapter, up_weight, band_start, band_len):
    half_rows = TOK_DEV // 2
    latent = jnp.dot(teacher.reshape(DOCS * TOKENS, TD), adapter, preferred_element_type=jnp.float32)
    latent = latent.astype(jnp.bfloat16).reshape(DOCS, TOKENS, RANK)
    latent_pad = jnp.pad(latent, ((0, 0), (half_rows, half_rows), (0, 0)))
    teacher_pad = jnp.pad(teacher, ((0, 0), (half_rows, half_rows), (0, 0)))

    def one_window(carry, index):
        doc_index = (index // N_SEQ).astype(jnp.int32)
        shard = (index % N_SEQ).astype(jnp.int32)
        offset = (shard * TOK_DEV).astype(jnp.int32)
        zero = jnp.zeros((), jnp.int32)
        key_rows = lax.dynamic_slice(latent_pad, (doc_index, offset, zero), (1, 2 * TOK_DEV, RANK))[0]
        wide_rows = lax.dynamic_slice(teacher_pad, (doc_index, offset, zero), (1, 2 * TOK_DEV, TD))[0]
        student_rows = lax.dynamic_slice(student, (doc_index, offset, zero), (1, TOK_DEV, SD))[0]
        firsts = lax.dynamic_slice(band_start, (doc_index, offset), (1, TOK_DEV))[0]
        lengths = lax.dynamic_slice(band_len, (doc_index, offset), (1, TOK_DEV))[0]
        row_first = (shard * TOK_DEV - half_rows).astype(jnp.int32)
        student_grad, key_grad, up_part, loss_part = band_pass(student_rows, key_rows, firsts, lengths, up_weight, row_first)
        adapter_part = contract_rows(wide_rows, key_grad)
        return (carry[0] + adapter_part, carry[1] + up_part, carry[2] + loss_part), student_grad

    start_carry = (jnp.zeros((TD, RANK), jnp.float32), jnp.zeros((RANK, SD), jnp.float32), jnp.zeros((), jnp.float32))
    totals, grads = lax.scan(one_window, start_carry, jnp.arange(DOCS * N_SEQ, dtype=jnp.int32))
    grad_scale = (DOCS * TOKENS) ** -0.5
    student_grad = grads.reshape(DOCS, TOKENS, SD)
    loss = totals[2] / (DOCS * TOKENS * SD)
    return student_grad, totals[0] * grad_scale, totals[1] * grad_scale, loss
```

```python
import functools

import jax
import jax.numpy as jnp
from jax import lax
from jax.experimental import pallas as pl
from jax.experimental.pallas import tpu as pltpu
from jax.sharding import Mesh
from jax.sharding import PartitionSpec as P

SEQ = ("seq_0", "seq_1")
SEQ_DOC = ("seq_0", "seq_1", "doc_0", "doc_1")
DOC = ("doc_0", "doc_1")
MESH_ID = pl.DeviceIdType.MESH
BF = jnp.bfloat16
F32 = jnp.float32


def dot(a, b):
    return jnp.dot(a, b, preferred_element_type=F32)


def near_first(n):
    return sorted(range(1, n), key=lambda k: (min(k, n - k), k))


def kernel(
    sizes,
    t_hbm, s_hbm, a_hbm, w_hbm, first_hbm, len_hbm,
    sg_hbm, ag_ref, ug_ref, loss_ref,
    A, T, TT, S, ST, W, WT, OGT, SG, FIRST, LEN, K, KS, KR,
    UPb, UCr, UXs, UXr, UT32, UZs, UZr, UYr, UGr,
    APb, ACr, AXs, AXr, AT32, AYs, AYr, AZs, AZr,
    LC, LZ, LY, LX,
    load_sem, out_sem,
    zc_s, zc_r, gy_s, gy_r, gx_s, gx_r, gc_s, gc_r,
    h_s, h_r, k_s, k_r,
    uc_s, uc_r, ux_s, ux_r, uz_s, uz_r, uy_s, uy_r, ug_s, ug_r,
    ac_s, ac_r, ax_s, ax_r, ay_s, ay_r, az_s, az_r,
    lc_s, lc_r, lz_s, lz_r, ly_s, ly_r, lx_s, lx_r,
):
    Y, X, Z, C, td, sd, tok, scale, grad_scale, loss_scale = sizes
    y = lax.axis_index("seq_0")
    x = lax.axis_index("seq_1")
    z = lax.axis_index("doc_0")
    c = lax.axis_index("doc_1")
    half = tok // 2
    blk = td // (Y * X)
    cut = blk // C
    xr = sd // (Z * C) // X
    yx = y * X + x

    def turn(v, k, n):
        return lax.rem(v + k, n) if k else v

    def dev(dy=0, dx=0, dz=0, dc=0):
        return (turn(y, dy, Y), turn(x, dx, X), turn(z, dz, Z), turn(c, dc, C))

    def beside(step):
        s = lax.rem(yx + step, Y * X)
        return (lax.div(s, X), lax.rem(s, X), z, c)

    right = beside(1)
    left = beside(Y * X - 1)
    sends = []

    def rcopy(src, dst, ss, rs, to):
        return pltpu.make_async_remote_copy(
            src_ref=src, dst_ref=dst, send_sem=ss, recv_sem=rs, device_id=to, device_id_type=MESH_ID
        )

    def send(src, dst, ss, rs, to):
        cp = rcopy(src, dst, ss, rs, to)
        cp.start()
        sends.append(cp)

    def arrived(dst, ss, rs, to):
        rcopy(dst, dst, ss, rs, to).wait_recv()

    zc_off = [(kz, kc) for kz in range(Z) for kc in range(C) if kz or kc]
    zc_off.sort(key=lambda k: (min(k[0], Z - k[0]), k))
    y_off, x_off, z_off = near_first(Y), near_first(X), near_first(Z)

    barrier = pltpu.get_barrier_semaphore()
    peers = [dev(dz=kz, dc=kc) for kz, kc in zc_off] + [dev(dy=k) for k in y_off]
    peers += [dev(dx=k) for k in x_off] + [left, right]
    for p in peers:
        pl.semaphore_signal(barrier, inc=1, device_id=p, device_id_type=MESH_ID)

    def own_rows(zz, cc):
        return pl.ds(pl.multiple_of((zz * C + cc) * 8, 8), 8)

    loads = [
        pltpu.make_async_copy(a_hbm, A.at[yx, own_rows(z, c)], load_sem.at[0]),
        pltpu.make_async_copy(s_hbm, S, load_sem.at[1]),
        pltpu.make_async_copy(w_hbm, W, load_sem.at[2]),
        pltpu.make_async_copy(t_hbm, T, load_sem.at[3]),
        pltpu.make_async_copy(first_hbm, FIRST, load_sem.at[4]),
        pltpu.make_async_copy(len_hbm, LEN, load_sem.at[5]),
    ]
    for cp in loads:
        cp.start()

    loads[1].wait()
    loads[2].wait()
    fb = 128
    for i in range(sd // fb):
        ST[i * fb:(i + 1) * fb, :] = S[:, i * fb:(i + 1) * fb].T
    query_t = dot(W[...], ST[...]).astype(BF)
    query = query_t.T
    loads[0].wait()
    pl.semaphore_wait(barrier, len(peers))

    mine = A.at[yx, own_rows(z, c)]
    for j, (kz, kc) in enumerate(zc_off):
        send(mine, mine, zc_s.at[j], zc_r.at[j], dev(dz=kz, dc=kc))
    for i in range(sd // fb):
        WT[i * fb:(i + 1) * fb, :] = W[:, i * fb:(i + 1) * fb].T
    loads[3].wait()
    for j, (kz, kc) in enumerate(zc_off):
        zz, cc = turn(z, Z - kz if kz else 0, Z), turn(c, C - kc if kc else 0, C)
        arrived(A.at[yx, own_rows(zz, cc)], zc_s.at[j], zc_r.at[j], dev())

    def part(yy, xx):
        return A.at[yy * X + xx, pl.ds(pl.multiple_of(c * cut, cut), cut)]

    def other_part(yy, xx):
        return A.at[yy * X + xx, pl.ds(pl.multiple_of((C - 1 - c) * cut, cut), cut)]

    for k in y_off:
        send(part(y, x), part(y, x), gy_s.at[k], gy_r.at[k], dev(dy=k))
    for m in x_off:
        send(part(y, x), part(y, x), gx_s.at[m], gx_r.at[m], dev(dx=m))
    nyx = td // fb
    for i in range(Y):
        for j in range(X):
            b = i * X + j
            TT[j, i] = T[:, b * blk:(b + 1) * blk].T
    for k in y_off:
        yy = turn(y, Y - k, Y)
        arrived(part(yy, x), gy_s.at[k], gy_r.at[k], dev())
        for m in x_off:
            send(part(yy, x), part(yy, x), gx_s.at[k * X + m], gx_r.at[k * X + m], dev(dx=m))
        send(part(yy, x), part(yy, x), gc_s.at[k * X], gc_r.at[k * X], dev(dc=1))
    for k in [0] + y_off:
        yy = turn(y, Y - k if k else 0, Y)
        for m in x_off:
            xx = turn(x, X - m, X)
            arrived(part(yy, xx), gx_s.at[k * X + m], gx_r.at[k * X + m], dev())
            send(part(yy, xx), part(yy, xx), gc_s.at[k * X + m], gc_r.at[k * X + m], dev(dc=1))
    for k in [0] + y_off:
        yy = turn(y, Y - k if k else 0, Y)
        for m in [0] + x_off:
            if k or m:
                xx = turn(x, X - m if m else 0, X)
                arrived(other_part(yy, xx), gc_s.at[k * X + m], gc_r.at[k * X + m], dev())

    K[half:half + tok, :] = dot(T[...], A[...].reshape(td, 128)).astype(BF)
    send(K.at[half:tok], K.at[half + tok:2 * tok], h_s.at[0], h_r.at[0], left)
    send(K.at[tok:half + tok], K.at[0:half], h_s.at[1], h_r.at[1], right)
    loads[4].wait()
    loads[5].wait()
    first = FIRST[...]
    past = first + LEN[...]
    position = yx * tok - half + lax.broadcasted_iota(jnp.int32, (2 * tok, tok), 0)
    inside = (position >= first) & (position < past)
    arrived(K.at[half + tok:2 * tok], h_s.at[0], h_r.at[0], left)
    arrived(K.at[0:half], h_s.at[1], h_r.at[1], right)

    keys = K[...]
    keys_t = keys.T
    scores = jnp.where(inside, dot(keys, query_t) * scale, -1e30)
    top = jnp.max(scores, axis=0, keepdims=True)
    weights = jnp.where(inside, jnp.exp(scores - top), 0.0)
    prob = weights / jnp.sum(weights, axis=0, keepdims=True)
    prob_b = prob.astype(BF)
    context_t = dot(keys_t, prob_b).astype(BF)
    loss_tile = jnp.zeros((8, tok), F32)
    ctx_grad_f = jnp.zeros((128, tok), F32)
    rb = 256
    for i in range(sd // rb):
        rows = slice(i * rb, (i + 1) * rb)
        res = ST[rows, :].astype(F32) - dot(WT[rows, :], context_t)
        loss_tile = loss_tile + jnp.sum((res * res).reshape(rb // 8, 8, tok), axis=0)
        og = (-res).astype(BF)
        OGT[rows, :] = og
        ctx_grad_f = ctx_grad_f + dot(W[:, rows], og)
    ctx_grad_t = ctx_grad_f.astype(BF)
    prob_grad = dot(keys, ctx_grad_t)
    centred = prob_grad - jnp.sum(prob * prob_grad, axis=0, keepdims=True)
    score_grad = (prob * centred * scale).astype(BF)
    KS[...] = (dot(prob_b, ctx_grad_t.T) + dot(score_grad, query)).astype(BF)
    send(KS.at[0:half], KR.at[half:tok], k_s.at[0], k_r.at[0], left)
    send(KS.at[half + tok:2 * tok], KR.at[0:half], k_s.at[1], k_r.at[1], right)
    query_grad = dot(keys_t, score_grad).astype(BF).T
    context = context_t.T

    for zi in range(Z):
        for ci in range(C):
            r0 = (zi * C + ci) * xr * X
            rows = slice(r0, r0 + xr * X)
            u = (dot(OGT[rows, :], context) + dot(ST[rows, :], query_grad)).astype(BF)
            for xi in range(X):
                UPb[ci, xi, zi] = u[xi * xr:(xi + 1) * xr, :]
    far_first = list(reversed(x_off))
    for k in far_first + [0]:
        xx = turn(x, k, X)
        send(UPb.at[C - 1 - c, xx], UCr.at[xx], uc_s.at[k], uc_r.at[k], dev(dc=1))
    LC[c] = loss_tile
    send(LC.at[c], LC.at[c], lc_s.at[0], lc_r.at[0], dev(dc=1))

    arrived(KR.at[half:tok], k_s.at[0], k_r.at[0], left)
    arrived(KR.at[0:half], k_s.at[1], k_r.at[1], right)
    pair = jnp.concatenate([KS[half:half + tok, :], KR[...]], axis=1)

    def adapter_terms(k):
        xx = turn(x, k, X)
        for i in range(Y):
            two = dot(TT[xx, i], pair)
            p = (two[:, :128] + two[:, 128:]).reshape(Z, C, 8, 128)
            for ci in range(C):
                APb[ci, xx, i] = p[:, ci].reshape(cut, 128).astype(BF)
        send(APb.at[C - 1 - c, xx], ACr.at[xx], ac_s.at[k], ac_r.at[k], dev(dc=1))

    def up_core_sum(k):
        xx = turn(x, k, X)
        arrived(UCr.at[xx], uc_s.at[k], uc_r.at[k], dev())
        return UPb[c, xx].astype(F32) + UCr[xx].astype(F32)

    def adapter_core_sum(k):
        xx = turn(x, k, X)
        arrived(ACr.at[xx], ac_s.at[k], ac_r.at[k], dev())
        return APb[c, xx].astype(F32) + ACr[xx].astype(F32)

    for k in far_first:
        UXs[k - 1] = up_core_sum(k).astype(BF)
        send(UXs.at[k - 1], UXr.at[k - 1], ux_s.at[k], ux_r.at[k], dev(dx=k))
        adapter_terms(k)
    adapter_terms(0)
    for k in far_first:
        AXs[k - 1] = adapter_core_sum(k).astype(BF)
        send(AXs.at[k - 1], AXr.at[k - 1], ax_s.at[k], ax_r.at[k], dev(dx=k))

    arrived(LC.at[C - 1 - c], lc_s.at[0], lc_r.at[0], dev())
    LZ[z] = jnp.sum(LC[...], axis=0)
    for k in z_off:
        send(LZ.at[z], LZ.at[z], lz_s.at[k], lz_r.at[k], dev(dz=k))

    for i in range(sd // rb):
        cols = slice(i * rb, (i + 1) * rb)
        wc = W[:, cols]
        res = S[:, cols].astype(F32) - dot(context, wc)
        SG[:, cols] = (res + dot(query_grad, wc)).astype(BF)
    sg_out = pltpu.make_async_copy(SG, sg_hbm, out_sem.at[0])
    sg_out.start()

    total = up_core_sum(0)
    for k in x_off:
        arrived(UXr.at[k - 1], ux_s.at[k], ux_r.at[k], dev())
        total = total + UXr[k - 1].astype(F32)
    UT32[...] = total
    UZs[...] = total.astype(BF)
    for k in z_off:
        send(UZs.at[turn(z, k, Z)], UZr.at[k - 1], uz_s.at[k], uz_r.at[k], dev(dz=k))
    total = adapter_core_sum(0)
    for k in x_off:
        arrived(AXr.at[k - 1], ax_s.at[k], ax_r.at[k], dev())
        total = total + AXr[k - 1].astype(F32)
    AT32[...] = total
    AYs[...] = total.astype(BF)
    for k in y_off:
        send(AYs.at[turn(y, k, Y)], AYr.at[k - 1], ay_s.at[k], ay_r.at[k], dev(dy=k))

    for k in z_off:
        arrived(LZ.at[turn(z, Z - k, Z)], lz_s.at[k], lz_r.at[k], dev())
    LY[y] = jnp.sum(LZ[...], axis=0)
    for k in y_off:
        send(LY.at[y], LY.at[y], ly_s.at[k], ly_r.at[k], dev(dy=k))

    total = UT32[z]
    for k in z_off:
        arrived(UZr.at[k - 1], uz_s.at[k], uz_r.at[k], dev())
        total = total + UZr[k - 1].astype(F32)
    UYr[y] = total.astype(BF)
    for k in y_off:
        send(UYr.at[y], UYr.at[y], uy_s.at[k], uy_r.at[k], dev(dy=k))
    total = AT32[y]
    for k in y_off:
        arrived(AYr.at[k - 1], ay_s.at[k], ay_r.at[k], dev())
        total = total + AYr[k - 1].astype(F32)
    AZs[...] = total.reshape(Z, 8, 128)
    for k in z_off:
        send(AZs.at[turn(z, k, Z)], AZr.at[k - 1], az_s.at[k], az_r.at[k], dev(dz=k))

    for k in y_off:
        arrived(LY.at[turn(y, Y - k, Y)], ly_s.at[k], ly_r.at[k], dev())
    LX[x] = jnp.sum(LY[...], axis=0)
    for k in x_off:
        send(LX.at[x], LX.at[x], lx_s.at[k], lx_r.at[k], dev(dx=k))

    for k in y_off:
        arrived(UYr.at[turn(y, Y - k, Y)], uy_s.at[k], uy_r.at[k], dev())
    UGr[x] = jnp.sum(UYr[...].astype(F32), axis=0) * grad_scale
    for k in x_off:
        send(UGr.at[x], UGr.at[x], ug_s.at[k], ug_r.at[k], dev(dx=k))
    total = AZs[z]
    for k in z_off:
        arrived(AZr.at[k - 1], az_s.at[k], az_r.at[k], dev())
        total = total + AZr[k - 1]
    ag_ref[...] = total * grad_scale
    for k in x_off:
        arrived(LX.at[turn(x, X - k, X)], lx_s.at[k], lx_r.at[k], dev())
    all_loss = jnp.sum(LX[...], axis=0)
    loss_ref[...] = jnp.sum(jnp.sum(all_loss, axis=0, keepdims=True), axis=1, keepdims=True) * loss_scale
    for k in x_off:
        arrived(UGr.at[turn(x, X - k, X)], ug_s.at[k], ug_r.at[k], dev())
    ug_ref[...] = UGr[...].reshape(xr * X, 128).T
    for cp in sends:
        cp.wait_send()
    sg_out.wait()


def on_device(shape, teacher, student, adapter, up_weight, band_start, band_len):
    Y, X, Z, C = shape
    _, tok, td = teacher.shape
    sd, rank = student.shape[2], adapter.shape[1]
    tokens = Y * X * Z * C * tok
    sizes = (Y, X, Z, C, td, sd, tok, sd ** (-0.5), tokens ** (-0.5), 0.5 / (tokens * sd))
    blk = td // (Y * X)
    cut = blk // C
    rw = sd // (Z * C)
    xr = rw // X
    V, D = pltpu.VMEM, pltpu.SemaphoreType.DMA
    buffers = [
        V((Y * X, blk, rank), BF), V((tok, td), BF), V((X, Y, blk, tok), BF),
        V((tok, sd), BF), V((sd, tok), BF), V((rank, sd), BF), V((sd, rank), BF), V((sd, tok), BF),
        V((tok, sd), BF), V((1, tok), jnp.int32), V((1, tok), jnp.int32),
        V((2 * tok, rank), BF), V((2 * tok, rank), BF), V((tok, rank), BF),
        V((C, X, Z, xr, rank), BF), V((X, Z, xr, rank), BF), V((X - 1, Z, xr, rank), BF),
        V((X - 1, Z, xr, rank), BF), V((Z, xr, rank), F32), V((Z, xr, rank), BF),
        V((Z - 1, xr, rank), BF), V((Y, xr, rank), BF), V((X, xr, rank), F32),
        V((C, X, Y, cut, rank), BF), V((X, Y, cut, rank), BF), V((X - 1, Y, cut, rank), BF),
        V((X - 1, Y, cut, rank), BF), V((Y, cut, rank), F32), V((Y, cut, rank), BF),
        V((Y - 1, cut, rank), BF), V((Z, 8, rank), F32), V((Z - 1, 8, rank), F32),
        V((C, 8, tok), F32), V((Z, 8, tok), F32), V((Y, 8, tok), F32), V((X, 8, tok), F32),
    ]
    counts = [Z * C, Y, Y * X, Y * X, 2, 2, X, X, Z, Y, X, X, X, Y, Z, 1, Z, Y, X]
    sems = [D((6,)), D((1,))]
    for n in counts:
        sems += [D((n,)), D((n,))]
    any_spec = pl.BlockSpec(memory_space=pl.ANY)
    vmem = pl.BlockSpec(memory_space=pltpu.VMEM)
    sg, ag, ug, loss = pl.pallas_call(
        functools.partial(kernel, sizes),
        out_shape=(
            jax.ShapeDtypeStruct((tok, sd), BF),
            jax.ShapeDtypeStruct((8, rank), F32),
            jax.ShapeDtypeStruct((rank, rw), F32),
            jax.ShapeDtypeStruct((1, 1), F32),
        ),
        in_specs=[any_spec] * 6,
        out_specs=(any_spec, vmem, vmem, vmem),
        scratch_shapes=buffers + sems,
        compiler_params=pltpu.CompilerParams(
            collective_id=0, has_side_effects=True, vmem_limit_bytes=60 * 2**20
        ),
    )(teacher[0], student[0], adapter, up_weight, band_start, band_len)
    return sg[None], ag, ug, loss[0, 0]


def build(torus):
    shape = tuple(torus.shape[a] for a in SEQ_DOC)
    placed = (P(DOC, SEQ, None), P(DOC, SEQ, None), P(SEQ_DOC, None), P(), P(DOC, SEQ), P(DOC, SEQ))
    return jax.shard_map(
        functools.partial(on_device, shape),
        mesh=torus,
        in_specs=placed,
        out_specs=(P(DOC, SEQ, None), P(SEQ_DOC, None), P(None, DOC), P()),
        check_vma=False,
    )


def solution(mesh):
    return build(Mesh(mesh.devices.reshape(8, 4, 8, 2), SEQ_DOC))
```
